256 devices in a mesh: dp: 16 (over x, y), head: 16 (over z, core).
Axes of the slice: x: 4, y: 4, z: 8, core: 2. Of those that a mesh axis runs over, the one named last changes fastest.
Arguments:
- latents: bfloat16 [2048, 512], P('dp'), may hold values from -6 to 6
- targets: bfloat16 [2048, 32768], P('dp', 'head'), may hold values from -6 to 6
- kv_weight: bfloat16 [512, 32768], P(None, 'head'), may hold values from -0.25 to 0.25
- momentum: float32 [512, 16, 2048], P(None, 'head', 'dp'), may hold values from -120 to 120
Outputs:
- momentum_out: float32 [512, 16, 2048], P(None, 'head', 'dp')
- update: float32 [512, 16, 2048], P(None, 'head', 'dp')
The draws below stay inside these ranges and needn't reach their ends.
All inputs are finite; a program needn't handle non-finite values.
Results may differ from the reference program's by a relative error of at most 0.0003.
The reference program's roundings to bfloat16 on the way (of `residual`) count: a program that leaves them out, or rounds other values in their place, can miss the bound.
Values may be sent and summed in bfloat16 or wider, within the bound.
A program may use at most 64 MiB of HBM per device.

```python
import math
import jax
import jax.numpy as jnp
from jax import lax

R = 512
C = 32768
ITERS = 2
TOKENS = 2048
SUB = 2048
N_HEAD = 16


def draw_momentum(key, part):
    key_base = jax.random.fold_in(key, 11)
    key_cols = jax.random.fold_in(key, 12)
    key_rows = jax.random.fold_in(key, 13)
    position = jnp.arange(C, dtype=jnp.float32) / C
    col_scale = jnp.exp(math.log(3.0) * position + jax.random.uniform(key_cols, (C,), jnp.float32, 0.0, math.log(4.0)))
    row_scale = jnp.exp(jax.random.uniform(key_rows, (R,), jnp.float32, 0.0, math.log(10.0)))
    base = jax.random.truncated_normal(key_base, -4.0, 4.0, (R, C), jnp.float32)
    values = 0.25 * base * row_scale[:, None] * col_scale[None, :]
    return values.reshape(R, N_HEAD, SUB).astype(jnp.float32)


def level_of(rng, dims, split, low, top_value):
    def one(dim, shards_of):
        heights = jax.random.uniform(jax.random.fold_in(jax.random.fold_in(rng, 6), dim), (shards_of,), jnp.float32, low / len(split), top_value / len(split))
        return jnp.repeat(jnp.exp(heights), dims[dim] // shards_of).reshape((-1,) + (1,) * (len(dims) - dim - 1))

    level = one(*split[0])
    for cut in split[1:]:
        level = level * one(*cut)
    return level


def bell_draw(own_key, dims, scale, most, split=(), kind=jnp.bfloat16):
    loudness = level_of(own_key, dims, split, -0.22, 0.18) if split else 1.0
    entries = jax.random.normal(own_key, dims, jnp.float32) * scale * loudness
    return jnp.minimum(jnp.maximum(entries, -most), most).astype(kind)


def setup_inputs(seed: int = 0) -> dict:
    seeds = jax.random.split(jax.random.key(seed), 5)
    return {
        "latents": bell_draw(seeds[0], (TOKENS, R), 1.0, 6.0, ((0, 16),)),
        "targets": bell_draw(seeds[1], (TOKENS, C), 1.0, 6.0, ((0, 16), (1, 16))),
        "kv_weight": bell_draw(seeds[2], (R, C), R ** -0.5, 0.25, ((1, 16),)),
        "momentum": draw_momentum(jax.random.fold_in(seeds[4], 71), 0),
    }


decay_rate = 0.95
linear_coef = 3.4445
square_coef = -4.775
quint_coef = 2.0315
epsilon = 1e-07

def reference(latents, targets, kv_weight, momentum):
    residual = (jnp.dot(latents, kv_weight, preferred_element_type=jnp.float32) - targets.astype(jnp.float32)).astype(jnp.bfloat16)
    gradient = jnp.dot(latents.T, residual, preferred_element_type=jnp.float32) * (1.0 / math.sqrt(TOKENS))
    previous = momentum.reshape(R, C)
    momentum_new = decay_rate * previous + gradient
    nesterov = gradient + decay_rate * momentum_new
    inverse = 1.0 / (jnp.sqrt(jnp.sum(nesterov * nesterov)) + epsilon)
    iterate = nesterov * inverse
    for iteration in range(ITERS):
        gram_matrix = jnp.dot(iterate, iterate.T, precision=lax.Precision.HIGHEST)
        polynomial = square_coef * gram_matrix + quint_coef * jnp.dot(gram_matrix, gram_matrix, precision=lax.Precision.HIGHEST)
        iterate = linear_coef * iterate + jnp.dot(polynomial, iterate, precision=lax.Precision.HIGHEST)
    update = iterate * math.sqrt(C)
    return (momentum_new.reshape(R, N_HEAD, SUB), update.reshape(R, N_HEAD, SUB))
```

```python
import math

import jax
import jax.numpy as jnp
from jax import lax
from jax.sharding import PartitionSpec as P

C = 32768

decay_rate = 0.95
linear_coef = 3.4445
square_coef = -4.775
quint_coef = 2.0315
epsilon = 1e-07
HIGHEST = lax.Precision.HIGHEST


def local(latents, targets, kv_weight, momentum):
    latent_width = momentum.shape[0]
    sub_width = momentum.shape[2]
    total_tokens = latents.shape[0] * lax.axis_size("dp")
    all_latents = lax.all_gather(latents, "dp", axis=0, tiled=True)
    my_targets = lax.all_to_all(targets, "dp", split_axis=1, concat_axis=0, tiled=True)
    start = lax.axis_index("dp") * sub_width
    my_weight = lax.dynamic_slice(kv_weight, (0, start), (latent_width, sub_width))
    residual = (
        jnp.dot(all_latents, my_weight, preferred_element_type=jnp.float32)
        - my_targets.astype(jnp.float32)
    ).astype(jnp.bfloat16)
    gradient = lax.dot_general(
        all_latents, residual, (((0,), (0,)), ((), ())), preferred_element_type=jnp.float32
    ) * (1.0 / math.sqrt(total_tokens))
    momentum_new = decay_rate * momentum.reshape(latent_width, sub_width) + gradient
    nesterov = gradient + decay_rate * momentum_new
    gram = lax.psum(
        lax.dot_general(nesterov, nesterov, (((1,), (1,)), ((), ())), precision=HIGHEST),
        ("dp", "head"),
    )
    inverse = 1.0 / (jnp.sqrt(jnp.trace(gram)) + epsilon)
    gram = gram * (inverse * inverse)
    eye = jnp.eye(latent_width, dtype=jnp.float32)
    first = linear_coef * eye + square_coef * gram + quint_coef * jnp.dot(gram, gram, precision=HIGHEST)
    second_gram = jnp.dot(first, jnp.dot(gram, first, precision=HIGHEST), precision=HIGHEST)
    second = (
        linear_coef * eye
        + square_coef * second_gram
        + quint_coef * jnp.dot(second_gram, second_gram, precision=HIGHEST)
    )
    iterate = jnp.dot(first, nesterov * (inverse * math.sqrt(C)), precision=HIGHEST)
    update = jnp.dot(second, iterate, precision=HIGHEST)
    return (
        momentum_new.reshape(latent_width, 1, sub_width),
        update.reshape(latent_width, 1, sub_width),
    )


def solution(mesh):
    return jax.shard_map(
        local,
        mesh=mesh,
        in_specs=(P("dp", None), P("dp", "head"), P(None, "head"), P(None, "head", "dp")),
        out_specs=(P(None, "head", "dp"), P(None, "head", "dp")),
        check_vma=False,
    )
```

```python
import functools
import math

import jax
import jax.numpy as jnp
from jax import lax
from jax.experimental import pallas as pl
from jax.experimental.pallas import tpu as pltpu
from jax.sharding import PartitionSpec as P

MESH = pl.DeviceIdType.MESH
F32, BF16 = jnp.float32, jnp.bfloat16

R = 512
C = 32768
TOKENS = 2048
NX = 4
NZ = 8
COLS = 128
HALF = 64
CHIPS = NX * NX
PIECE = 5 * 128 // CHIPS

decay_rate = 0.95
linear_coef = 3.4445
square_coef = -4.775
quint_coef = 2.0315
epsilon = 1e-07

OFFSETS = [(0, 1), (0, 3), (1, 0), (3, 0), (1, 1), (1, 3), (3, 1), (3, 3), (0, 2), (2, 0), (1, 2), (3, 2), (2, 1), (2, 3), (2, 2)]
RING = (1, 3, 2)
ZRING = (4, 3, 5, 2, 6, 1, 7)
BLOCKS = (((0, 0), (0, 1), (1, 1), (0, 2), (0, 3)), ((2, 2), (2, 3), (3, 3), (1, 2), (1, 3)))


def split(value):
    high = value.astype(BF16)
    return high, (value - high.astype(F32)).astype(BF16)


def dot(a, b):
    return jnp.dot(a, b, preferred_element_type=F32)


def dot_nt(a, b):
    return lax.dot_general(a, b, (((1,), (1,)), ((), ())), preferred_element_type=F32)


def dot_tn(a, b):
    return lax.dot_general(a, b, (((0,), (0,)), ((), ())), preferred_element_type=F32)


def multiply(a, b):
    (ah, al), (bh, bl) = a, b
    return dot(ah, bh) + (dot(ah, bl) + dot(al, bh))


def kernel(
    lat, tgt, wgt, mom, mom_out, upd_out,
    lbuf, tbuf, wbuf, mbuf, gown, gsib, xbuf, gs, rbuf, pz, zbuf, gf, gm, mh, ml, ph, pl_lo, qh, ql, pm,
    send_a, send_b, local_sem, sem_l, sem_t, sem_w, sem_m, sem_g, sem_r, sem_z, sem_f, sem_s,
):
    chip = lax.axis_index("dp")
    head = lax.axis_index("head")
    x, y = lax.div(chip, NX), lax.rem(chip, NX)
    z, c = lax.div(head, 2), lax.rem(head, 2)
    sibling = (chip, z * 2 + (1 - c))
    p1 = jnp.where(c == 0, y, x)
    p2 = jnp.where(c == 0, x, y)
    stride1 = jnp.where(c == 0, 1, NX)
    stride2 = jnp.where(c == 0, NX, 1)

    def step(p, by):
        return lax.rem(p + by, NX)

    def ring1(by):
        return (step(p1, by) * stride1 + p2 * stride2, head)

    def ring2(by):
        return (p1 * stride1 + step(p2, by) * stride2, head)

    def plane(offset):
        return step(x, offset[0]) * NX + step(y, offset[1])

    my_cols = pl.ds(pl.multiple_of(c * COLS, COLS), COLS)
    block_cols = pl.ds(pl.multiple_of(chip * COLS, COLS), COLS)
    my_slot = p2 * NX + p1

    def remote(src, dst, ssem, rsem, device):
        return pltpu.make_async_remote_copy(
            src_ref=src, dst_ref=dst, send_sem=ssem, recv_sem=rsem, device_id=device, device_id_type=MESH
        )

    local = [
        pltpu.make_async_copy(wgt.at[:, block_cols], wbuf.at[:, my_cols], local_sem.at[0]),
        pltpu.make_async_copy(lat.at[pl.ds(pl.multiple_of(c * HALF, HALF), HALF)], lbuf.at[my_slot], local_sem.at[1]),
        pltpu.make_async_copy(
            tgt.at[pl.ds(pl.multiple_of(c * HALF, HALF), HALF), block_cols], tbuf.at[my_slot, :, my_cols], local_sem.at[2]
        ),
        pltpu.make_async_copy(mom, mbuf.at[:, my_cols], local_sem.at[3]),
    ]
    for copy in local:
        copy.start()

    barrier = pltpu.get_barrier_semaphore()
    partners = 0
    for offset in OFFSETS:
        for core in range(2):
            pl.semaphore_signal(barrier, inc=1, device_id=(plane(offset), z * 2 + core), device_id_type=MESH)
            partners += 1
    for by in ZRING:
        pl.semaphore_signal(barrier, inc=1, device_id=(chip, lax.rem(z + by, NZ) * 2 + c), device_id_type=MESH)
        partners += 1
    pl.semaphore_signal(barrier, inc=1, device_id=sibling, device_id_type=MESH)
    pl.semaphore_wait(barrier, partners + 1)

    sends = []
    count_a = [0]

    def send_now(src, dst, rsem, device):
        copy = remote(src, dst, send_a.at[count_a[0]], rsem, device)
        count_a[0] += 1
        copy.start()
        sends.append(copy)

    my_half = lat.at[pl.ds(pl.multiple_of(c * HALF, HALF), HALF)]
    for by in RING:
        send_now(my_half, lbuf.at[my_slot], sem_l.at[my_slot], ring1(by))
    for by in RING:
        send_now(my_half, lbuf.at[my_slot], sem_l.at[my_slot], ring2(by))
    slot_on = (x * NX + y, y * NX + x)
    for offset in OFFSETS:
        to = plane(offset)
        to_cols = pl.ds(pl.multiple_of(to * COLS, COLS), COLS)
        for core in range(2):
            send_now(
                tgt.at[pl.ds(core * HALF, HALF), to_cols],
                tbuf.at[slot_on[core], :, my_cols],
                sem_t.at[slot_on[core]],
                (to, z * 2 + core),
            )
    sib_slot = p1 * NX + p2
    send_now(wgt.at[:, block_cols], wbuf.at[:, my_cols], sem_w, sibling)
    send_now(
        tgt.at[pl.ds(pl.multiple_of((1 - c) * HALF, HALF), HALF), block_cols],
        tbuf.at[sib_slot, :, my_cols],
        sem_t.at[sib_slot],
        sibling,
    )
    send_now(mom, mbuf.at[:, my_cols], sem_m, sibling)

    def wait_recv(ref, sem):
        remote(ref, ref, send_a.at[0], sem, sibling).wait_recv()

    for by in RING:
        slot = p2 * NX + step(p1, by)
        wait_recv(lbuf.at[slot], sem_l.at[slot])
        for by2 in RING:
            send_now(lbuf.at[slot], lbuf.at[slot], sem_l.at[slot], ring2(by2))

    sib_cols = pl.ds(pl.multiple_of((1 - c) * COLS, COLS), COLS)
    for copy in local:
        copy.wait()
    wait_recv(wbuf.at[:, sib_cols], sem_w)
    weight = wbuf[...]

    for group, by in enumerate((0,) + RING):
        q2 = step(p2, by)
        for by1 in (0,) + RING:
            slot = q2 * NX + step(p1, by1)
            if by == 0 and by1 == 0:
                wait_recv(tbuf.at[slot, :, sib_cols], sem_t.at[slot])
            else:
                wait_recv(tbuf.at[slot], sem_t.at[slot])
            if by != 0:
                wait_recv(lbuf.at[slot], sem_l.at[slot])
        tokens = NX * HALF
        latent = lbuf[pl.ds(q2 * NX, NX)].reshape(tokens, R)
        target = tbuf[pl.ds(q2 * NX, NX)].reshape(tokens, 2 * COLS)
        residual = (dot(latent, weight) - target.astype(F32)).astype(BF16)
        part = dot_tn(latent, residual)
        if group == 0:
            gown[...] = part
        else:
            gown[...] += part

    exchange = remote(gown, gsib, send_b.at[0], sem_g, sibling)
    exchange.start()
    wait_recv(mbuf.at[:, sib_cols], sem_m)
    exchange.wait_recv()
    gradient = (gown[...] + gsib[...]) * (1.0 / math.sqrt(TOKENS))
    momentum_new = decay_rate * mbuf[...] + gradient
    nesterov = gradient + decay_rate * momentum_new
    mbuf[...] = momentum_new
    gsib[...] = nesterov
    xbuf[0], xbuf[1] = split(nesterov)
    mom_out[...] = mbuf[:, my_cols]

    def rows(start, size):
        at = pl.ds(pl.multiple_of(start, 128), size)
        return xbuf[0, at, :], xbuf[1, at, :]

    def gram(a, b):
        (ah, al), (bh, bl) = a, b
        return dot_nt(ah, bh) + (dot_nt(ah, bl) + dot_nt(al, bh))

    square = rows(c * 256, 256)
    diagonal = gram(square, square)
    gs[0:128, :] = diagonal[:128, :128]
    gs[128:256, :] = diagonal[:128, 128:]
    gs[256:384, :] = diagonal[128:, 128:]
    upper = gram(rows(c * 128, 128), rows(256, 256))
    gs[384:512, :] = upper[:, :128]
    gs[512:640, :] = upper[:, 128:]

    def piece(of):
        return pl.ds(pl.multiple_of(of * PIECE, 8), PIECE)

    count_b = [1]

    def send_b_now(src, dst, rsem, device):
        copy = remote(src, dst, send_b.at[count_b[0]], rsem, device)
        count_b[0] += 1
        copy.start()
        sends.append(copy)

    for k, offset in reversed(list(enumerate(OFFSETS))):
        to = plane(offset)
        send_b_now(gs.at[piece(to)], rbuf.at[k], sem_r, (to, head))
    wait_recv(rbuf, sem_r)
    total = gs[piece(chip), :]
    for k in range(CHIPS - 1):
        total = total + rbuf[k]
    pz[...] = total
    for by in ZRING:
        send_b_now(pz, zbuf.at[by - 1], sem_z, (chip, lax.rem(z + by, NZ) * 2 + c))
    wait_recv(zbuf, sem_z)
    for k in range(NZ - 1):
        total = total + zbuf[k]
    gf[c, piece(chip), :] = total
    for k, offset in reversed(list(enumerate(OFFSETS))):
        send_b_now(gf.at[c, piece(chip)], gf.at[c, piece(chip)], sem_f.at[k], (plane(offset), head))
    send_b_now(gf.at[c, piece(chip)], gf.at[c, piece(chip)], sem_s, sibling)
    for k, offset in enumerate(OFFSETS):
        source = plane(((4 - offset[0]) % 4, (4 - offset[1]) % 4))
        wait_recv(gf.at[c, piece(source)], sem_f.at[k])
        send_b_now(gf.at[c, piece(source)], gf.at[c, piece(source)], sem_s, sibling)
    wait_recv(gf.at[1 - c], sem_s)

    line = lax.broadcasted_iota(jnp.int32, (128, 128), 0)
    column = lax.broadcasted_iota(jnp.int32, (128, 128), 1)
    diag = line == column
    trace = jnp.zeros((1, 1), F32)
    for half in range(2):
        both = gf[half, 0:128, :] + gf[half, 256:384, :]
        trace = trace + jnp.sum(jnp.where(diag, both, 0.0), keepdims=True)
    inverse = 1.0 / (jnp.sqrt(trace) + epsilon)
    inverse2 = inverse * inverse
    for half in range(2):
        for index, (i, j) in enumerate(BLOCKS[half]):
            block = gf[half, index * 128 : (index + 1) * 128, :] * inverse2
            gm[i * 128 : (i + 1) * 128, j * 128 : (j + 1) * 128] = block
            if i != j:
                gm[j * 128 : (j + 1) * 128, i * 128 : (i + 1) * 128] = block.T
    eye_line = lax.broadcasted_iota(jnp.int32, (R, R), 0)
    eye_column = lax.broadcasted_iota(jnp.int32, (R, R), 1)
    identity = jnp.where(eye_line == eye_column, linear_coef, 0.0).astype(F32)

    mh[...], ml[...] = split(gm[...])
    first = identity + square_coef * gm[...] + quint_coef * multiply((mh[...], ml[...]), (mh[...], ml[...]))
    ph[...], pl_lo[...] = split(first)
    iterate = gsib[:, my_cols] * (inverse * math.sqrt(C))
    iterate = multiply((ph[...], pl_lo[...]), split(iterate))
    qh[...], ql[...] = split(multiply((ph[...], pl_lo[...]), (mh[...], ml[...])))
    pm[...] = multiply((qh[...], ql[...]), (ph[...], pl_lo[...]))
    mh[...], ml[...] = split(pm[...])
    second = identity + square_coef * pm[...] + quint_coef * multiply((mh[...], ml[...]), (mh[...], ml[...]))
    ph[...], pl_lo[...] = split(second)
    upd_out[...] = multiply((ph[...], pl_lo[...]), split(iterate))

    for copy in sends:
        copy.wait_send()
    exchange.wait_send()


def local(latents, targets, kv_weight, momentum):
    previous = momentum.reshape(R, COLS)
    dma = pltpu.SemaphoreType.DMA
    any_space = pl.BlockSpec(memory_space=pl.ANY)
    vmem = pl.BlockSpec(memory_space=pltpu.VMEM)
    momentum_new, update = pl.pallas_call(
        kernel,
        out_shape=(jax.ShapeDtypeStruct((R, COLS), F32), jax.ShapeDtypeStruct((R, COLS), F32)),
        in_specs=[any_space] * 4,
        out_specs=(vmem, vmem),
        scratch_shapes=[
            pltpu.VMEM((CHIPS, HALF, R), BF16),
            pltpu.VMEM((CHIPS, HALF, 2 * COLS), BF16),
            pltpu.VMEM((R, 2 * COLS), BF16),
            pltpu.VMEM((R, 2 * COLS), F32),
            pltpu.VMEM((R, 2 * COLS), F32),
            pltpu.VMEM((R, 2 * COLS), F32),
            pltpu.VMEM((2, R, 2 * COLS), BF16),
            pltpu.VMEM((5 * 128, 128), F32),
            pltpu.VMEM((CHIPS - 1, PIECE, 128), F32),
            pltpu.VMEM((PIECE, 128), F32),
            pltpu.VMEM((NZ - 1, PIECE, 128), F32),
            pltpu.VMEM((2, 5 * 128, 128), F32),
            pltpu.VMEM((R, R), F32),
            pltpu.VMEM((R, R), BF16),
            pltpu.VMEM((R, R), BF16),
            pltpu.VMEM((R, R), BF16),
            pltpu.VMEM((R, R), BF16),
            pltpu.VMEM((R, R), BF16),
            pltpu.VMEM((R, R), BF16),
            pltpu.VMEM((R, R), F32),
            dma((48,)),
            dma((56,)),
            dma((4,)),
            dma((CHIPS,)),
            dma((CHIPS,)),
            dma,
            dma,
            dma,
            dma,
            dma,
            dma((CHIPS - 1,)),
            dma,
        ],
        compiler_params=pltpu.CompilerParams(
            collective_id=0, has_side_effects=True, vmem_limit_bytes=56 << 20
        ),
        name="muon_step",
    )(latents, targets, kv_weight, previous)
    return momentum_new.reshape(R, 1, COLS), update.reshape(R, 1, COLS)


def solution(mesh):
    return jax.shard_map(
        local,
        mesh=mesh,
        in_specs=(P("dp", None), P("dp", "head"), P(None, "head"), P(None, "head", "dp")),
        out_specs=(P(None, "head", "dp"), P(None, "head", "dp")),
        check_vma=False,
    )
```

```python
import math

import jax
import jax.numpy as jnp
from jax import lax
from jax.experimental import pallas as pl
from jax.experimental.pallas import tpu as pltpu
from jax.sharding import PartitionSpec as P

MESH = pl.DeviceIdType.MESH
F32, BF16 = jnp.float32, jnp.bfloat16

R = 512
C = 32768
TOKENS = 2048
NX = 4
NZ = 8
COLS = 128
HALF = 64
QUARTER = 32
CHIPS = NX * NX
PIECE = 5 * 128 // CHIPS
CHUNK = 256

decay_rate = 0.95
linear_coef = 3.4445
square_coef = -4.775
quint_coef = 2.0315
epsilon = 1e-07

OFFSETS = [(0, 1), (0, 3), (1, 0), (3, 0), (1, 1), (1, 3), (3, 1), (3, 3), (0, 2), (2, 0), (1, 2), (3, 2), (2, 1), (2, 3), (2, 2)]
FAR_FIRST = list(reversed(list(enumerate(OFFSETS))))
RING = (1, 3, 2)
ZRING = (4, 3, 5, 2, 6, 1, 7)
BLOCKS = (((0, 0), (256, 256)), ((0, 128), (256, 256)), ((128, 128), (256, 256)), ((0, 256), (128, 0)), ((0, 384), (128, 0)))


def split(value):
    high = value.astype(BF16)
    return high, (value - high.astype(F32)).astype(BF16)


def dot(a, b):
    return jnp.dot(a, b, preferred_element_type=F32)


def dot_nt(a, b):
    return lax.dot_general(a, b, (((1,), (1,)), ((), ())), preferred_element_type=F32)


def dot_tn(a, b):
    return lax.dot_general(a, b, (((0,), (0,)), ((), ())), preferred_element_type=F32)


def kernel(
    lat, tgt, wgt, mom, mom_out, upd_out,
    lbuf, tstage, tbuf, wbuf, mbuf, gown, gsib, xbuf, nest, gs, rbuf, pz, zbuf, gf, gm, gh, gl, ph, plo,
    send_a, send_b, local_sem, sem_l, sem_lz, sem_t, sem_w, sem_m, sem_g, sem_r, sem_z, sem_f, sem_s, out_sem, ready,
):
    chip = lax.axis_index("dp")
    head = lax.axis_index("head")
    x, y = lax.div(chip, NX), lax.rem(chip, NX)
    z, c = lax.div(head, 2), lax.rem(head, 2)
    sibling = (chip, z * 2 + (1 - c))

    def step(p, by):
        return lax.rem(p + by, NX)

    def along_z(by):
        return (chip, lax.rem(z + by, NZ) * 2 + c)

    def plane(offset):
        return step(x, offset[0]) * NX + step(y, offset[1])

    def remote(src, dst, ssem, rsem, device):
        return pltpu.make_async_remote_copy(
            src_ref=src, dst_ref=dst, send_sem=ssem, recv_sem=rsem, device_id=device, device_id_type=MESH
        )

    def wait_recv(ref, sem):
        remote(ref, ref, send_a.at[0], sem, sibling).wait_recv()

    barrier = pltpu.get_barrier_semaphore()
    partners = 1
    for by in ZRING:
        pl.semaphore_signal(barrier, inc=1, device_id=along_z(by), device_id_type=MESH)
        partners += 1
    for _, offset in FAR_FIRST:
        pl.semaphore_signal(barrier, inc=1, device_id=(plane(offset), head), device_id_type=MESH)
        partners += 1
    pl.semaphore_signal(barrier, inc=1, device_id=sibling, device_id_type=MESH)

    zp = lax.rem(z, 2)
    block_cols = pl.ds(pl.multiple_of(chip * COLS, COLS), COLS)

    def quarter(of):
        return lat.at[pl.ds(pl.multiple_of(c * HALF + of * QUARTER, QUARTER), QUARTER)]

    for to in range(CHIPS):
        pltpu.make_async_copy(tgt.at[:, to * COLS : (to + 1) * COLS], tstage.at[to], local_sem.at[0]).start()
    own_weight = pltpu.make_async_copy(wgt.at[:, block_cols], wbuf.at[0], local_sem.at[1])
    own_weight.start()
    own_quarter = pltpu.make_async_copy(quarter(zp), lbuf.at[chip, zp], local_sem.at[2])
    own_quarter.start()
    pltpu.make_async_copy(quarter(1 - zp), lbuf.at[chip, 1 - zp], sem_lz.at[x]).start()
    own_momentum = pltpu.make_async_copy(mom, mbuf.at[0], local_sem.at[3])
    own_momentum.start()
    pl.semaphore_wait(barrier, partners)
    pl.semaphore_signal(ready, inc=1, device_id=sibling, device_id_type=MESH)

    sends = []
    count_a = [0]

    def send_now(src, dst, rsem, device):
        copy = remote(src, dst, send_a.at[count_a[0]], rsem, device)
        count_a[0] += 1
        copy.start()
        sends.append(copy)

    for _, offset in FAR_FIRST:
        send_now(quarter(zp), lbuf.at[chip, zp], sem_l.at[chip], (plane(offset), head))

    pltpu.make_async_copy(tstage, tstage, local_sem.at[0]).wait()
    my_rows = pl.ds(pl.multiple_of(c * HALF, HALF), HALF)
    sib_rows = pl.ds(pl.multiple_of((1 - c) * HALF, HALF), HALF)
    for _, offset in FAR_FIRST:
        to = plane(offset)
        send_now(tstage.at[to, my_rows], tbuf.at[0, chip], sem_t.at[x], (to, head))
    pl.semaphore_wait(ready, 1)
    for _, offset in FAR_FIRST:
        to = plane(offset)
        send_now(tstage.at[to, sib_rows], tbuf.at[1, chip], sem_t.at[x], (to, z * 2 + (1 - c)))
    own_weight.wait()
    send_now(wbuf.at[0], wbuf.at[1], sem_w, sibling)
    send_now(tstage.at[chip, sib_rows], tbuf.at[1, chip], sem_t.at[x], sibling)
    send_now(mom, mbuf.at[1], sem_m, sibling)
    pltpu.make_async_copy(tstage.at[chip, my_rows], tbuf.at[0, chip], sem_t.at[x]).start()

    flip = [0]

    def swap(slot):
        side = 1 if flip[0] % 2 == 0 else NZ - 1
        flip[0] += 1
        send_now(lbuf.at[slot, zp], lbuf.at[slot, zp], sem_lz.at[lax.div(slot, NX)], along_z(side))

    for offset in OFFSETS:
        slot = plane(offset)
        wait_recv(lbuf.at[slot, zp], sem_l.at[slot])
        swap(slot)

    own_quarter.wait()
    wait_recv(wbuf.at[1], sem_w)
    tokens = NX * HALF

    def group_of(by):
        return pl.ds(step(x, by) * NX, NX)

    def residual_of(by):
        group = group_of(by)
        wait_recv(tbuf.at[:, group], sem_t.at[step(x, by)])
        wait_recv(lbuf.at[group, 1 - zp], sem_lz.at[step(x, by)])
        weight = jnp.concatenate([wbuf[0], wbuf[1]], axis=1)
        target = jnp.concatenate([tbuf[0, group].reshape(tokens, COLS), tbuf[1, group].reshape(tokens, COLS)], axis=1)
        return (dot(lbuf[group].reshape(tokens, R), weight) - target.astype(F32)).astype(BF16)

    def add_gradient(by, residual, first):
        latent = lbuf[group_of(by)].reshape(tokens, R)
        part = dot_tn(latent, residual)
        for r in range(2):
            value = part[:, r * COLS : (r + 1) * COLS]
            if first:
                gown[r] = value
            else:
                gown[r] += value

    add_gradient(0, residual_of(0), True)
    add_gradient(1, residual_of(1), False)
    add_gradient(3, residual_of(3), False)

    residual = residual_of(2)
    for chunk in range(R // CHUNK):
        at = slice(chunk * CHUNK, (chunk + 1) * CHUNK)
        part = dot_tn(lbuf[group_of(2), :, :, at].reshape(tokens, CHUNK), residual)
        for r in range(2):
            gown[r, at, :] += part[:, r * COLS : (r + 1) * COLS]
            send_now(gown.at[r, at], gsib.at[1 - r, at], sem_g.at[chunk, r], sibling)
    wait_recv(mbuf.at[1], sem_m)
    own_momentum.wait()
    for chunk in range(R // CHUNK):
        at = slice(chunk * CHUNK, (chunk + 1) * CHUNK)
        for r in range(2):
            wait_recv(gsib.at[r, at], sem_g.at[chunk, 1 - r])
            gradient = (gown[r, at, :] + gsib[r, at, :]) * (1.0 / math.sqrt(TOKENS))
            momentum_new = decay_rate * mbuf[r, at, :] + gradient
            nesterov = gradient + decay_rate * momentum_new
            if r == 0:
                mbuf[0, at, :] = momentum_new
                nest[at, :] = nesterov
            xbuf[0, at, r * COLS : (r + 1) * COLS], xbuf[1, at, r * COLS : (r + 1) * COLS] = split(nesterov)
    momentum_done = pltpu.make_async_copy(mbuf.at[0], mom_out, out_sem)
    momentum_done.start()

    def rows(start, size):
        at = pl.ds(pl.multiple_of(start, 128), size)
        return xbuf[0, at, :], xbuf[1, at, :]

    def gram(a, b):
        (ah, al), (bh, bl) = a, b
        return dot_nt(ah, bh) + (dot_nt(ah, bl) + dot_nt(al, bh))

    square = rows(c * 256, 256)
    diagonal = gram(square, square)
    gs[0:128, :] = diagonal[:128, :128]
    gs[128:256, :] = diagonal[:128, 128:]
    gs[256:384, :] = diagonal[128:, 128:]
    upper = gram(rows(c * 128, 128), rows(256, 256))
    gs[384:512, :] = upper[:, :128]
    gs[512:640, :] = upper[:, 128:]

    def piece(of):
        return pl.ds(pl.multiple_of(of * PIECE, 8), PIECE)

    count_b = [0]

    def send_b_now(src, dst, rsem, device):
        copy = remote(src, dst, send_b.at[count_b[0]], rsem, device)
        count_b[0] += 1
        copy.start()
        sends.append(copy)

    for k, offset in FAR_FIRST:
        to = plane(offset)
        send_b_now(gs.at[piece(to)], rbuf.at[k], sem_r, (to, head))
    wait_recv(rbuf, sem_r)
    total = gs[piece(chip), :]
    for k in range(CHIPS - 1):
        total = total + rbuf[k]
    pz[...] = total
    for by in ZRING:
        send_b_now(pz, zbuf.at[by - 1], sem_z, along_z(by))
    wait_recv(zbuf, sem_z)
    for k in range(NZ - 1):
        total = total + zbuf[k]
    gf[c, piece(chip), :] = total
    for k, offset in FAR_FIRST:
        send_b_now(gf.at[c, piece(chip)], gf.at[c, piece(chip)], sem_f.at[k], (plane(offset), head))
    send_b_now(gf.at[c, piece(chip)], gf.at[c, piece(chip)], sem_s, sibling)
    for k, offset in enumerate(OFFSETS):
        source = plane(((4 - offset[0]) % 4, (4 - offset[1]) % 4))
        wait_recv(gf.at[c, piece(source)], sem_f.at[k])
        send_b_now(gf.at[c, piece(source)], gf.at[c, piece(source)], sem_s, sibling)

    def place(half):
        for index, (base, more) in enumerate(BLOCKS):
            line = pl.ds(pl.multiple_of(base[0] + half * more[0], 128), 128)
            column = pl.ds(pl.multiple_of(base[1] + half * more[1], 128), 128)
            block = gf[half, index * 128 : (index + 1) * 128, :]
            gm[line, column] = block
            gh[line, column], gl[line, column] = split(block)
            if index not in (0, 2):
                block = block.T
                gm[column, line] = block
                gh[column, line], gl[column, line] = split(block)

    place(c)
    wait_recv(gf.at[1 - c], sem_s)
    place(1 - c)
    diag = lax.broadcasted_iota(jnp.int32, (128, 128), 0) == lax.broadcasted_iota(jnp.int32, (128, 128), 1)
    both = (gf[0, 0:128, :] + gf[0, 256:384, :]) + (gf[1, 0:128, :] + gf[1, 256:384, :])
    trace = jnp.sum(jnp.where(diag, both, 0.0), keepdims=True)
    inverse = 1.0 / (jnp.sqrt(trace) + epsilon)
    inverse2 = inverse * inverse

    for chunk in range(R // CHUNK):
        at = slice(chunk * CHUNK, (chunk + 1) * CHUNK)
        squared = dot(gh[at, :], gh[...]) + (dot(gh[at, :], gl[...]) + dot(gl[at, :], gh[...]))
        line = lax.broadcasted_iota(jnp.int32, (CHUNK, R), 0) + chunk * CHUNK
        column = lax.broadcasted_iota(jnp.int32, (CHUNK, R), 1)
        polynomial = jnp.where(line == column, linear_coef, 0.0).astype(F32) + (
            square_coef * gm[at, :] + (quint_coef * squared) * inverse2
        ) * inverse2
        ph[at, :], plo[at, :] = split(polynomial)

    def apply(high, low, vector):
        vh, vl = split(vector)
        wide = dot(high[...], jnp.concatenate([vh, vl], axis=1))
        return wide[:, :COLS] + (wide[:, COLS:] + dot(low[...], vh))

    def apply_second(vector):
        vector = apply(ph, plo, vector)
        vector = apply(gh, gl, vector) * inverse2
        return apply(ph, plo, vector)

    iterate = apply(ph, plo, nest[...] * (inverse * math.sqrt(C)))
    once = apply_second(iterate)
    twice = apply_second(once)
    upd_out[...] = linear_coef * iterate + (square_coef * once + quint_coef * twice)

    momentum_done.wait()
    for copy in sends:
        copy.wait_send()


def finish(mom_ref, upd_ref, mom_out, upd_out, held, sems):
    pairs = ((mom_ref, mom_out), (upd_ref, upd_out))
    loads = [pltpu.make_async_copy(source, held.at[i], sems.at[0, i]) for i, (source, _) in enumerate(pairs)]
    stores = [pltpu.make_async_copy(held.at[i], target, sems.at[1, i]) for i, (_, target) in enumerate(pairs)]
    for load in loads:
        load.start()
    for load, store in zip(loads, stores):
        load.wait()
        store.start()
    for store in stores:
        store.wait()


def local(latents, targets, kv_weight, momentum):
    previous = momentum.reshape(R, COLS)
    dma = pltpu.SemaphoreType.DMA
    any_space = pl.BlockSpec(memory_space=pl.ANY)
    vmem = pl.BlockSpec(memory_space=pltpu.VMEM)
    matrix = jax.ShapeDtypeStruct((R, COLS), F32)
    momentum_new, update = pl.pallas_call(
        kernel,
        out_shape=(matrix, matrix),
        in_specs=[any_space] * 4,
        out_specs=(any_space, vmem),
        scratch_shapes=[
            pltpu.VMEM((CHIPS, 2, QUARTER, R), BF16),
            pltpu.VMEM((CHIPS, 2 * HALF, COLS), BF16),
            pltpu.VMEM((2, CHIPS, HALF, COLS), BF16),
            pltpu.VMEM((2, R, COLS), BF16),
            pltpu.VMEM((2, R, COLS), F32),
            pltpu.VMEM((2, R, COLS), F32),
            pltpu.VMEM((2, R, COLS), F32),
            pltpu.VMEM((2, R, 2 * COLS), BF16),
            pltpu.VMEM((R, COLS), F32),
            pltpu.VMEM((5 * 128, 128), F32),
            pltpu.VMEM((CHIPS - 1, PIECE, 128), F32),
            pltpu.VMEM((PIECE, 128), F32),
            pltpu.VMEM((NZ - 1, PIECE, 128), F32),
            pltpu.VMEM((2, 5 * 128, 128), F32),
            pltpu.VMEM((R, R), F32),
            pltpu.VMEM((R, R), BF16),
            pltpu.VMEM((R, R), BF16),
            pltpu.VMEM((R, R), BF16),
            pltpu.VMEM((R, R), BF16),
            dma((72,)),
            dma((56,)),
            dma((4,)),
            dma((CHIPS,)),
            dma((NX,)),
            dma((NX,)),
            dma,
            dma,
            dma((R // CHUNK, 2)),
            dma,
            dma,
            dma((CHIPS - 1,)),
            dma,
            dma,
            pltpu.SemaphoreType.REGULAR,
        ],
        compiler_params=pltpu.CompilerParams(
            collective_id=0, has_side_effects=True, vmem_limit_bytes=56 << 20
        ),
        name="muon_step",
    )(latents, targets, kv_weight, previous)
    momentum_new, update = pl.pallas_call(
        finish,
        out_shape=(matrix, matrix),
        in_specs=[any_space] * 2,
        out_specs=(any_space, any_space),
        scratch_shapes=[pltpu.VMEM((2, R, COLS), F32), dma((2, 2))],
        name="finish",
    )(momentum_new, update)
    return momentum_new.reshape(R, 1, COLS), update.reshape(R, 1, COLS)


def solution(mesh):
    return jax.shard_map(
        local,
        mesh=mesh,
        in_specs=(P("dp", None), P("dp", "head"), P(None, "head"), P(None, "head", "dp")),
        out_specs=(P(None, "head", "dp"), P(None, "head", "dp")),
        check_vma=False,
    )
```

```python
import math

import jax
import jax.numpy as jnp
from jax import lax
from jax.experimental import pallas as pl
from jax.experimental.pallas import tpu as pltpu
from jax.sharding import PartitionSpec as P

MESH = pl.DeviceIdType.MESH
F32, BF16 = jnp.float32, jnp.bfloat16

R = 512
C = 32768
TOKENS = 2048
NX = 4
NZ = 8
COLS = 128
HALF = 64
QUARTER = 32
CHIPS = NX * NX
PARTS = ((0, 3 * 128), (3 * 128, 2 * 128))
CHUNK = 256

decay_rate = 0.95
linear_coef = 3.4445
square_coef = -4.775
quint_coef = 2.0315
epsilon = 1e-07

OFFSETS = [(0, 1), (0, 3), (1, 0), (3, 0), (1, 1), (1, 3), (3, 1), (3, 3), (0, 2), (2, 0), (1, 2), (3, 2), (2, 1), (2, 3), (2, 2)]
FAR_FIRST = list(reversed(list(enumerate(OFFSETS))))
RING = (1, 3, 2)
ZRING = (4, 3, 5, 2, 6, 1, 7)
BLOCKS = (((0, 0), (256, 256)), ((0, 128), (256, 256)), ((128, 128), (256, 256)), ((0, 256), (128, 0)), ((0, 384), (128, 0)))


def split(value):
    high = value.astype(BF16)
    return high, (value - high.astype(F32)).astype(BF16)


def dot(a, b):
    return jnp.dot(a, b, preferred_element_type=F32)


def dot_nt(a, b):
    return lax.dot_general(a, b, (((1,), (1,)), ((), ())), preferred_element_type=F32)


def dot_tn(a, b):
    return lax.dot_general(a, b, (((0,), (0,)), ((), ())), preferred_element_type=F32)


def kernel(
    lat, tgt, wgt, mom, mom_out, upd_out,
    lbuf, tstage, tbuf, wbuf, mbuf, gown, gsib, xbuf, nest, gs, rbuf0, rbuf1, pz0, pz1, zbuf0, zbuf1, gf, gm, gh, gl, ph, plo,
    send_a, send_b, local_sem, sem_l, sem_lz, sem_t, sem_w, sem_m, sem_g, sem_r, sem_z, sem_f, sem_s, out_sem, ready, ubuf, upd_sem, word,
):
    chip = lax.axis_index("dp")
    head = lax.axis_index("head")
    x, y = lax.div(chip, NX), lax.rem(chip, NX)
    z, c = lax.div(head, 2), lax.rem(head, 2)
    sibling = (chip, z * 2 + (1 - c))

    def step(p, by):
        return lax.rem(p + by, NX)

    def along_z(by):
        return (chip, lax.rem(z + by, NZ) * 2 + c)

    def plane(offset):
        return step(x, offset[0]) * NX + step(y, offset[1])

    def remote(src, dst, ssem, rsem, device):
        return pltpu.make_async_remote_copy(
            src_ref=src, dst_ref=dst, send_sem=ssem, recv_sem=rsem, device_id=device, device_id_type=MESH
        )

    def wait_recv(ref, sem):
        remote(ref, ref, send_a.at[0], sem, sibling).wait_recv()

    barrier = pltpu.get_barrier_semaphore()
    partners = 1
    for _, offset in FAR_FIRST:
        pl.semaphore_signal(barrier, inc=1, device_id=(plane(offset), head), device_id_type=MESH)
        partners += 1
    for by in (1, NZ - 1):
        pl.semaphore_signal(barrier, inc=1, device_id=along_z(by), device_id_type=MESH)
        partners += 1
    pl.semaphore_signal(barrier, inc=1, device_id=sibling, device_id_type=MESH)

    zp = lax.rem(z, 2)
    block_cols = pl.ds(pl.multiple_of(chip * COLS, COLS), COLS)

    def quarter(of):
        return lat.at[pl.ds(pl.multiple_of(c * HALF + of * QUARTER, QUARTER), QUARTER)]

    own_quarter = pltpu.make_async_copy(quarter(zp), lbuf.at[chip, zp], local_sem.at[2])
    own_quarter.start()
    for to in range(CHIPS):
        pltpu.make_async_copy(tgt.at[:, to * COLS : (to + 1) * COLS], tstage.at[to], local_sem.at[0]).start()
    own_weight = pltpu.make_async_copy(wgt.at[:, block_cols], wbuf.at[0], local_sem.at[1])
    own_weight.start()
    pltpu.make_async_copy(quarter(1 - zp), lbuf.at[chip, 1 - zp], sem_lz.at[x]).start()
    own_momentum = pltpu.make_async_copy(mom, mbuf.at[0], local_sem.at[3])
    own_momentum.start()
    pl.semaphore_wait(barrier, partners)
    pl.semaphore_signal(ready, inc=1, device_id=sibling, device_id_type=MESH)

    def tell_z(turn):
        pl.semaphore_signal(word.at[turn, 0], inc=1, device_id=along_z(1), device_id_type=MESH)
        pl.semaphore_signal(word.at[turn, 1], inc=1, device_id=along_z(NZ - 1), device_id_type=MESH)

    def hear_z(turn):
        pl.semaphore_wait(word.at[turn, 0], 1)
        pl.semaphore_wait(word.at[turn, 1], 1)

    sends = []
    count_a = [0]

    def send_now(src, dst, rsem, device):
        copy = remote(src, dst, send_a.at[count_a[0]], rsem, device)
        count_a[0] += 1
        copy.start()
        sends.append(copy)

    own_quarter.wait()
    for _, offset in FAR_FIRST:
        send_now(lbuf.at[chip, zp], lbuf.at[chip, zp], sem_l.at[chip], (plane(offset), head))

    pltpu.make_async_copy(tstage, tstage, local_sem.at[0]).wait()
    my_rows = pl.ds(pl.multiple_of(c * HALF, HALF), HALF)
    sib_rows = pl.ds(pl.multiple_of((1 - c) * HALF, HALF), HALF)
    for _, offset in FAR_FIRST:
        to = plane(offset)
        send_now(tstage.at[to, my_rows], tbuf.at[0, chip], sem_t.at[x], (to, head))
    tell_z(0)
    pl.semaphore_wait(ready, 1)
    for _, offset in FAR_FIRST:
        to = plane(offset)
        send_now(tstage.at[to, sib_rows], tbuf.at[1, chip], sem_t.at[x], (to, z * 2 + (1 - c)))
    own_weight.wait()
    send_now(wbuf.at[0], wbuf.at[1], sem_w, sibling)
    send_now(tstage.at[chip, sib_rows], tbuf.at[1, chip], sem_t.at[x], sibling)
    send_now(mom, mbuf.at[1], sem_m, sibling)
    pltpu.make_async_copy(tstage.at[chip, my_rows], tbuf.at[0, chip], sem_t.at[x]).start()

    flip = [0]

    def swap(slot):
        side = 1 if flip[0] % 2 == 0 else NZ - 1
        flip[0] += 1
        send_now(lbuf.at[slot, zp], lbuf.at[slot, zp], sem_lz.at[lax.div(slot, NX)], along_z(side))

    for offset in OFFSETS:
        slot = plane(offset)
        wait_recv(lbuf.at[slot, zp], sem_l.at[slot])
        swap(slot)

    hear_z(0)
    tell_z(1)
    wait_recv(wbuf.at[1], sem_w)
    tokens = NX * HALF

    def group_of(by):
        return pl.ds(step(x, by) * NX, NX)

    def residual_of(by):
        group = group_of(by)
        wait_recv(tbuf.at[:, group], sem_t.at[step(x, by)])
        wait_recv(lbuf.at[group, 1 - zp], sem_lz.at[step(x, by)])
        weight = jnp.concatenate([wbuf[0], wbuf[1]], axis=1)
        target = jnp.concatenate([tbuf[0, group].reshape(tokens, COLS), tbuf[1, group].reshape(tokens, COLS)], axis=1)
        return (dot(lbuf[group].reshape(tokens, R), weight) - target.astype(F32)).astype(BF16)

    def add_gradient(by, residual, first):
        latent = lbuf[group_of(by)].reshape(tokens, R)
        part = dot_tn(latent, residual)
        for r in range(2):
            value = part[:, r * COLS : (r + 1) * COLS]
            if first:
                gown[r] = value
            else:
                gown[r] += value

    add_gradient(0, residual_of(0), True)
    hear_z(1)
    tell_z(2)
    add_gradient(1, residual_of(1), False)
    add_gradient(3, residual_of(3), False)

    residual = residual_of(2)

    def chunk_at(of):
        return pl.ds(pl.multiple_of(of * CHUNK, CHUNK), CHUNK)

    for order, at in enumerate((chunk_at(1 - c), chunk_at(c))):
        part = dot_tn(lbuf[group_of(2), :, :, at].reshape(tokens, CHUNK), residual)
        for r in range(2):
            gown[r, at, :] += part[:, r * COLS : (r + 1) * COLS]
            send_now(gown.at[r, at], gsib.at[1 - r, at], sem_g.at[order, r], sibling)
    wait_recv(mbuf.at[1], sem_m)
    own_momentum.wait()

    def nesterov_of(order, at):
        for r in range(2):
            wait_recv(gsib.at[r, at], sem_g.at[order, 1 - r])
            gradient = (gown[r, at, :] + gsib[r, at, :]) * (1.0 / math.sqrt(TOKENS))
            momentum_new = decay_rate * mbuf[r, at, :] + gradient
            nesterov = gradient + decay_rate * momentum_new
            if r == 0:
                mbuf[0, at, :] = momentum_new
                nest[at, :] = nesterov
            xbuf[0, at, r * COLS : (r + 1) * COLS], xbuf[1, at, r * COLS : (r + 1) * COLS] = split(nesterov)

    def rows(start, size):
        at = pl.ds(pl.multiple_of(start, 128), size)
        return xbuf[0, at, :], xbuf[1, at, :]

    def gram(a, b):
        (ah, al), (bh, bl) = a, b
        return dot_nt(ah, bh) + (dot_nt(ah, bl) + dot_nt(al, bh))

    def piece(part, of):
        size = PARTS[part][1] // CHIPS
        return pl.ds(pl.multiple_of(PARTS[part][0] + of * size, 8), size)

    count_b = [0]

    def send_b_now(src, dst, rsem, device):
        copy = remote(src, dst, send_b.at[count_b[0]], rsem, device)
        count_b[0] += 1
        copy.start()
        sends.append(copy)

    received, summed, over_z = (rbuf0, rbuf1), (pz0, pz1), (zbuf0, zbuf1)

    def scatter(part):
        for k, offset in FAR_FIRST:
            to = plane(offset)
            send_b_now(gs.at[piece(part, to)], received[part].at[k], sem_r.at[part], (to, head))

    hear_z(2)
    nesterov_of(0, chunk_at(c))
    square = rows(c * CHUNK, CHUNK)
    diagonal = gram(square, square)
    gs[0:128, :] = diagonal[:128, :128]
    gs[128:256, :] = diagonal[:128, 128:]
    gs[256:384, :] = diagonal[128:, 128:]
    scatter(0)
    nesterov_of(1, chunk_at(1 - c))
    upper = gram(rows(c * 128, 128), rows(256, 256))
    gs[384:512, :] = upper[:, :128]
    gs[512:640, :] = upper[:, 128:]
    scatter(1)
    momentum_done = pltpu.make_async_copy(mbuf.at[0], mom_out, out_sem)
    momentum_done.start()

    for part in range(2):
        wait_recv(received[part], sem_r.at[part])
        total = gs[piece(part, chip), :]
        for k in range(CHIPS - 1):
            total = total + received[part][k]
        summed[part][...] = total
        for by in ZRING:
            send_b_now(summed[part], over_z[part].at[by - 1], sem_z.at[part], along_z(by))
    for part in range(2):
        wait_recv(over_z[part], sem_z.at[part])
        total = summed[part][...]
        for k in range(NZ - 1):
            total = total + over_z[part][k]
        mine = gf.at[c, piece(part, chip)]
        gf[c, piece(part, chip), :] = total
        for k, offset in FAR_FIRST:
            send_b_now(mine, mine, sem_f.at[part, k], (plane(offset), head))
        send_b_now(mine, mine, sem_s.at[part], sibling)

    def place(half, part):
        for index in ((0, 1, 2), (3, 4))[part]:
            base, more = BLOCKS[index]
            line = pl.ds(pl.multiple_of(base[0] + half * more[0], 128), 128)
            column = pl.ds(pl.multiple_of(base[1] + half * more[1], 128), 128)
            block = gf[half, index * 128 : (index + 1) * 128, :]
            gm[line, column] = block
            gh[line, column], gl[line, column] = split(block)
            if index not in (0, 2):
                block = block.T
                gm[column, line] = block
                gh[column, line], gl[column, line] = split(block)

    for part in range(2):
        for k, offset in enumerate(OFFSETS):
            source = gf.at[c, piece(part, plane(((4 - offset[0]) % 4, (4 - offset[1]) % 4)))]
            wait_recv(source, sem_f.at[part, k])
            send_b_now(source, source, sem_s.at[part], sibling)
        place(c, part)
    for part in range(2):
        start, size = PARTS[part]
        wait_recv(gf.at[1 - c, start : start + size], sem_s.at[part])
        place(1 - c, part)

    diag = lax.broadcasted_iota(jnp.int32, (128, 128), 0) == lax.broadcasted_iota(jnp.int32, (128, 128), 1)
    both = (gf[0, 0:128, :] + gf[0, 256:384, :]) + (gf[1, 0:128, :] + gf[1, 256:384, :])
    trace = jnp.sum(jnp.where(diag, both, 0.0), keepdims=True)
    inverse = 1.0 / (jnp.sqrt(trace) + epsilon)
    inverse2 = inverse * inverse

    for chunk in range(R // CHUNK):
        at = slice(chunk * CHUNK, (chunk + 1) * CHUNK)
        squared = dot(gh[at, :], gh[...]) + (dot(gh[at, :], gl[...]) + dot(gl[at, :], gh[...]))
        line = lax.broadcasted_iota(jnp.int32, (CHUNK, R), 0) + chunk * CHUNK
        column = lax.broadcasted_iota(jnp.int32, (CHUNK, R), 1)
        polynomial = jnp.where(line == column, linear_coef, 0.0).astype(F32) + (
            square_coef * gm[at, :] + (quint_coef * squared) * inverse2
        ) * inverse2
        ph[at, :], plo[at, :] = split(polynomial)

    def apply(high, low, vector):
        vh, vl = split(vector)
        wide = dot(high[...], jnp.concatenate([vh, vl], axis=1))
        return wide[:, :COLS] + (wide[:, COLS:] + dot(low[...], vh))

    def apply_second(vector):
        vector = apply(ph, plo, vector)
        vector = apply(gh, gl, vector) * inverse2
        return apply(ph, plo, vector)

    iterate = apply(ph, plo, nest[...] * (inverse * math.sqrt(C)))
    once = apply_second(iterate)
    twice = apply_second(once)
    ubuf[...] = linear_coef * iterate + (square_coef * once + quint_coef * twice)

    update_done = pltpu.make_async_copy(ubuf, upd_out, upd_sem)
    update_done.start()
    momentum_done.wait()
    update_done.wait()
    for copy in sends:
        copy.wait_send()


def finish(mom_ref, upd_ref, mom_out, upd_out, sems):
    stores = [
        pltpu.make_async_copy(mom_ref, mom_out, sems.at[0]),
        pltpu.make_async_copy(upd_ref, upd_out, sems.at[1]),
    ]
    for store in stores:
        store.start()
    for store in stores:
        store.wait()


def local(latents, targets, kv_weight, momentum):
    previous = momentum.reshape(R, COLS)
    dma = pltpu.SemaphoreType.DMA
    any_space = pl.BlockSpec(memory_space=pl.ANY)
    vmem = pl.BlockSpec(memory_space=pltpu.VMEM)
    matrix = jax.ShapeDtypeStruct((R, COLS), F32)
    momentum_new, update = pl.pallas_call(
        kernel,
        out_shape=(matrix, matrix),
        in_specs=[any_space] * 4,
        out_specs=(any_space, any_space),
        scratch_shapes=[
            pltpu.VMEM((CHIPS, 2, QUARTER, R), BF16),
            pltpu.VMEM((CHIPS, 2 * HALF, COLS), BF16),
            pltpu.VMEM((2, CHIPS, HALF, COLS), BF16),
            pltpu.VMEM((2, R, COLS), BF16),
            pltpu.VMEM((2, R, COLS), F32),
            pltpu.VMEM((2, R, COLS), F32),
            pltpu.VMEM((2, R, COLS), F32),
            pltpu.VMEM((2, R, 2 * COLS), BF16),
            pltpu.VMEM((R, COLS), F32),
            pltpu.VMEM((5 * 128, 128), F32),
            *[pltpu.VMEM((CHIPS - 1, size // CHIPS, 128), F32) for _, size in PARTS],
            *[pltpu.VMEM((size // CHIPS, 128), F32) for _, size in PARTS],
            *[pltpu.VMEM((NZ - 1, size // CHIPS, 128), F32) for _, size in PARTS],
            pltpu.VMEM((2, 5 * 128, 128), F32),
            pltpu.VMEM((R, R), F32),
            pltpu.VMEM((R, R), BF16),
            pltpu.VMEM((R, R), BF16),
            pltpu.VMEM((R, R), BF16),
            pltpu.VMEM((R, R), BF16),
            dma((72,)),
            dma((112,)),
            dma((4,)),
            dma((CHIPS,)),
            dma((NX,)),
            dma((NX,)),
            dma,
            dma,
            dma((2, 2)),
            dma((2,)),
            dma((2,)),
            dma((2, CHIPS - 1)),
            dma((2,)),
            dma,
            pltpu.SemaphoreType.REGULAR,
            pltpu.VMEM((R, COLS), F32),
            dma,
            pltpu.SemaphoreType.REGULAR((3, 2)),
        ],
        compiler_params=pltpu.CompilerParams(
            collective_id=0, has_side_effects=True, vmem_limit_bytes=32 << 20
        ),
        name="muon_step",
    )(*[pltpu.with_memory_space_constraint(v, pltpu.HBM) for v in (latents, targets, kv_weight, previous)])
    momentum_new, update = pl.pallas_call(
        finish,
        out_shape=(matrix, matrix),
        in_specs=[vmem] * 2,
        out_specs=(any_space, any_space),
        scratch_shapes=[dma((2,))],
        compiler_params=pltpu.CompilerParams(vmem_limit_bytes=4 << 20),
        name="finish",
    )(momentum_new, update)
    return momentum_new.reshape(R, 1, COLS), update.reshape(R, 1, COLS)


def solution(mesh):
    return jax.shard_map(
        local,
        mesh=mesh,
        in_specs=(P("dp", None), P("dp", "head"), P(None, "head"), P(None, "head", "dp")),
        out_specs=(P(None, "head", "dp"), P(None, "head", "dp")),
        check_vma=False,
    )
```

```python
import math

import jax
import jax.numpy as jnp
from jax import lax
from jax.experimental import pallas as pl
from jax.experimental.pallas import tpu as pltpu
from jax.sharding import PartitionSpec as P

MESH = pl.DeviceIdType.MESH
F32, BF16 = jnp.float32, jnp.bfloat16

R = 512
C = 32768
TOKENS = 2048
NX = 4
NZ = 8
COLS = 128
HALF = 64
QUARTER = 32
CHIPS = NX * NX
PARTS = ((0, 3 * 128), (3 * 128, 2 * 128))
CHUNK = 256

decay_rate = 0.95
linear_coef = 3.4445
square_coef = -4.775
quint_coef = 2.0315
epsilon = 1e-07

OFFSETS = [(0, 1), (0, 3), (1, 0), (3, 0), (1, 1), (1, 3), (3, 1), (3, 3), (0, 2), (2, 0), (1, 2), (3, 2), (2, 1), (2, 3), (2, 2)]
FAR_FIRST = list(reversed(list(enumerate(OFFSETS))))
DIRECT = ((0, 2), (2, 0), (0, 1), (0, 3), (1, 0), (3, 0))
RING = (1, 3, 2)
ZRING = (4, 3, 5, 2, 6, 1, 7)
BLOCKS = (((0, 0), (256, 256)), ((0, 128), (256, 256)), ((128, 128), (256, 256)), ((0, 256), (128, 0)), ((0, 384), (128, 0)))


def split(value):
    high = value.astype(BF16)
    return high, (value - high.astype(F32)).astype(BF16)


def dot(a, b):
    return jnp.dot(a, b, preferred_element_type=F32)


def dot_nt(a, b):
    return lax.dot_general(a, b, (((1,), (1,)), ((), ())), preferred_element_type=F32)


def dot_tn(a, b):
    return lax.dot_general(a, b, (((0,), (0,)), ((), ())), preferred_element_type=F32)


def kernel(
    lat, tgt, wgt, mom, mom_out, upd_out,
    lbuf, tstage, tbuf, wbuf, mbuf, gown, gsib, xbuf, nest, gs, rbuf0, rbuf1, pz0, pz1, zbuf0, zbuf1, gf, gm, gh, gl, ph, plo,
    send_a, send_b, local_sem, sem_l, sem_lz, sem_t, sem_w, sem_m, sem_g, sem_r, sem_z, sem_f, sem_s, out_sem, ready, word,
):
    chip = lax.axis_index("dp")
    head = lax.axis_index("head")
    x, y = lax.div(chip, NX), lax.rem(chip, NX)
    z, c = lax.div(head, 2), lax.rem(head, 2)
    sibling = (chip, z * 2 + (1 - c))

    def step(p, by):
        return lax.rem(p + by, NX)

    def along_z(by):
        return (chip, lax.rem(z + by, NZ) * 2 + c)

    def plane(offset):
        return step(x, offset[0]) * NX + step(y, offset[1])

    def turned(offset):
        a = jnp.where(c == 0, offset[0], offset[1])
        b = jnp.where(c == 0, offset[1], offset[0])
        return plane((a, b))

    def remote(src, dst, ssem, rsem, device):
        return pltpu.make_async_remote_copy(
            src_ref=src, dst_ref=dst, send_sem=ssem, recv_sem=rsem, device_id=device, device_id_type=MESH
        )

    def wait_recv(ref, sem):
        remote(ref, ref, send_a.at[0], sem, sibling).wait_recv()

    barrier = pltpu.get_barrier_semaphore()
    partners = 1
    for _, offset in FAR_FIRST:
        pl.semaphore_signal(barrier, inc=1, device_id=(plane(offset), head), device_id_type=MESH)
        partners += 1
    for by in (1, NZ - 1):
        pl.semaphore_signal(barrier, inc=1, device_id=along_z(by), device_id_type=MESH)
        partners += 1
    pl.semaphore_signal(barrier, inc=1, device_id=sibling, device_id_type=MESH)

    zp = lax.rem(z, 2)
    block_cols = pl.ds(pl.multiple_of(chip * COLS, COLS), COLS)

    def quarter(of):
        return lat.at[pl.ds(pl.multiple_of(c * HALF + of * QUARTER, QUARTER), QUARTER)]

    own_quarter = pltpu.make_async_copy(quarter(zp), lbuf.at[chip, zp], local_sem.at[2])
    own_quarter.start()
    for to in range(CHIPS):
        pltpu.make_async_copy(tgt.at[:, to * COLS : (to + 1) * COLS], tstage.at[to], local_sem.at[0]).start()
    own_weight = pltpu.make_async_copy(wgt.at[:, block_cols], wbuf.at[0], local_sem.at[1])
    own_weight.start()
    pltpu.make_async_copy(quarter(1 - zp), lbuf.at[chip, 1 - zp], sem_lz.at[x]).start()
    own_momentum = pltpu.make_async_copy(mom, mbuf.at[0], local_sem.at[3])
    own_momentum.start()
    pl.semaphore_wait(barrier, partners)
    pl.semaphore_signal(ready, inc=1, device_id=sibling, device_id_type=MESH)

    def tell_z(turn):
        pl.semaphore_signal(word.at[turn, 0], inc=1, device_id=along_z(1), device_id_type=MESH)
        pl.semaphore_signal(word.at[turn, 1], inc=1, device_id=along_z(NZ - 1), device_id_type=MESH)

    def hear_z(turn):
        pl.semaphore_wait(word.at[turn, 0], 1)
        pl.semaphore_wait(word.at[turn, 1], 1)

    sends = []
    count_a = [0]

    def send_now(src, dst, rsem, device):
        copy = remote(src, dst, send_a.at[count_a[0]], rsem, device)
        count_a[0] += 1
        copy.start()
        sends.append(copy)

    own_quarter.wait()
    for offset in DIRECT:
        send_now(lbuf.at[chip, zp], lbuf.at[chip, zp], sem_l.at[chip], (turned(offset), head))

    pltpu.make_async_copy(tstage, tstage, local_sem.at[0]).wait()
    my_rows = pl.ds(pl.multiple_of(c * HALF, HALF), HALF)
    sib_rows = pl.ds(pl.multiple_of((1 - c) * HALF, HALF), HALF)
    own_weight.wait()
    send_now(wbuf.at[0], wbuf.at[1], sem_w, sibling)
    send_now(tstage.at[chip, sib_rows], tbuf.at[1, chip], sem_t.at[x], sibling)
    send_now(mom, mbuf.at[1], sem_m, sibling)
    pltpu.make_async_copy(tstage.at[chip, my_rows], tbuf.at[0, chip], sem_t.at[x]).start()

    flip = [0]

    def swap(slot):
        side = 1 if flip[0] % 2 == 0 else NZ - 1
        flip[0] += 1
        send_now(lbuf.at[slot, zp], lbuf.at[slot, zp], sem_lz.at[lax.div(slot, NX)], along_z(side))

    def arrival(offset, passed_to=()):
        slot = turned(offset)
        wait_recv(lbuf.at[slot, zp], sem_l.at[slot])
        for onward in passed_to:
            send_now(lbuf.at[slot, zp], lbuf.at[slot, zp], sem_l.at[slot], (turned(onward), head))
        swap(slot)

    arrival((0, 1), ((1, 0), (3, 0)))
    arrival((0, 3), ((1, 0), (3, 0)))
    arrival((0, 2), ((2, 0), (1, 0), (3, 0)))
    arrival((2, 0), ((0, 1), (0, 3)))
    arrival((1, 0))
    arrival((3, 0))
    for _, offset in FAR_FIRST:
        to = plane(offset)
        send_now(tstage.at[to, my_rows], tbuf.at[0, chip], sem_t.at[x], (to, head))
    tell_z(0)
    pl.semaphore_wait(ready, 1)
    for _, offset in FAR_FIRST:
        to = plane(offset)
        send_now(tstage.at[to, sib_rows], tbuf.at[1, chip], sem_t.at[x], (to, z * 2 + (1 - c)))
    for offset in OFFSETS[4:8] + OFFSETS[10:]:
        arrival(offset)

    hear_z(0)
    tell_z(1)
    wait_recv(wbuf.at[1], sem_w)
    tokens = NX * HALF

    def group_of(by):
        return pl.ds(step(x, by) * NX, NX)

    def residual_of(by):
        group = group_of(by)
        wait_recv(tbuf.at[:, group], sem_t.at[step(x, by)])
        wait_recv(lbuf.at[group, 1 - zp], sem_lz.at[step(x, by)])
        weight = jnp.concatenate([wbuf[0], wbuf[1]], axis=1)
        target = jnp.concatenate([tbuf[0, group].reshape(tokens, COLS), tbuf[1, group].reshape(tokens, COLS)], axis=1)
        return (dot(lbuf[group].reshape(tokens, R), weight) - target.astype(F32)).astype(BF16)

    def add_gradient(by, residual, first):
        latent = lbuf[group_of(by)].reshape(tokens, R)
        part = dot_tn(latent, residual)
        for r in range(2):
            value = part[:, r * COLS : (r + 1) * COLS]
            if first:
                gown[r] = value
            else:
                gown[r] += value

    add_gradient(0, residual_of(0), True)
    hear_z(1)
    tell_z(2)
    add_gradient(1, residual_of(1), False)
    add_gradient(3, residual_of(3), False)

    residual = residual_of(2)

    def chunk_at(of):
        return pl.ds(pl.multiple_of(of * CHUNK, CHUNK), CHUNK)

    for order, at in enumerate((chunk_at(1 - c), chunk_at(c))):
        part = dot_tn(lbuf[group_of(2), :, :, at].reshape(tokens, CHUNK), residual)
        for r in range(2):
            gown[r, at, :] += part[:, r * COLS : (r + 1) * COLS]
            send_now(gown.at[r, at], gsib.at[1 - r, at], sem_g.at[order, r], sibling)
    wait_recv(mbuf.at[1], sem_m)
    own_momentum.wait()

    def nesterov_of(order, at):
        for r in range(2):
            wait_recv(gsib.at[r, at], sem_g.at[order, 1 - r])
            gradient = (gown[r, at, :] + gsib[r, at, :]) * (1.0 / math.sqrt(TOKENS))
            momentum_new = decay_rate * mbuf[r, at, :] + gradient
            nesterov = gradient + decay_rate * momentum_new
            if r == 0:
                mbuf[0, at, :] = momentum_new
                nest[at, :] = nesterov
            xbuf[0, at, r * COLS : (r + 1) * COLS], xbuf[1, at, r * COLS : (r + 1) * COLS] = split(nesterov)

    def rows(start, size):
        at = pl.ds(pl.multiple_of(start, 128), size)
        return xbuf[0, at, :], xbuf[1, at, :]

    def gram(a, b):
        (ah, al), (bh, bl) = a, b
        return dot_nt(ah, bh) + (dot_nt(ah, bl) + dot_nt(al, bh))

    def piece(part, of):
        size = PARTS[part][1] // CHIPS
        return pl.ds(pl.multiple_of(PARTS[part][0] + of * size, 8), size)

    count_b = [0]

    def send_b_now(src, dst, rsem, device):
        copy = remote(src, dst, send_b.at[count_b[0]], rsem, device)
        count_b[0] += 1
        copy.start()
        sends.append(copy)

    received, summed, over_z = (rbuf0, rbuf1), (pz0, pz1), (zbuf0, zbuf1)

    def scatter(part):
        for k, offset in FAR_FIRST:
            to = plane(offset)
            send_b_now(gs.at[piece(part, to)], received[part].at[k], sem_r.at[part], (to, head))

    hear_z(2)
    nesterov_of(0, chunk_at(c))
    square = rows(c * CHUNK, CHUNK)
    diagonal = gram(square, square)
    gs[0:128, :] = diagonal[:128, :128]
    gs[128:256, :] = diagonal[:128, 128:]
    gs[256:384, :] = diagonal[128:, 128:]
    scatter(0)
    nesterov_of(1, chunk_at(1 - c))
    upper = gram(rows(c * 128, 128), rows(256, 256))
    gs[384:512, :] = upper[:, :128]
    gs[512:640, :] = upper[:, 128:]
    scatter(1)
    momentum_done = pltpu.make_async_copy(mbuf.at[0], mom_out, out_sem)
    momentum_done.start()

    for part in range(2):
        wait_recv(received[part], sem_r.at[part])
        total = gs[piece(part, chip), :]
        for k in range(CHIPS - 1):
            total = total + received[part][k]
        summed[part][...] = total
        for by in ZRING:
            send_b_now(summed[part], over_z[part].at[by - 1], sem_z.at[part], along_z(by))
    for part in range(2):
        wait_recv(over_z[part], sem_z.at[part])
        total = summed[part][...]
        for k in range(NZ - 1):
            total = total + over_z[part][k]
        mine = gf.at[c, piece(part, chip)]
        gf[c, piece(part, chip), :] = total
        for k, offset in FAR_FIRST:
            send_b_now(mine, mine, sem_f.at[part, k], (plane(offset), head))
        send_b_now(mine, mine, sem_s.at[part], sibling)

    def place(half, part):
        for index in ((0, 1, 2), (3, 4))[part]:
            base, more = BLOCKS[index]
            line = pl.ds(pl.multiple_of(base[0] + half * more[0], 128), 128)
            column = pl.ds(pl.multiple_of(base[1] + half * more[1], 128), 128)
            block = gf[half, index * 128 : (index + 1) * 128, :]
            gm[line, column] = block
            gh[line, column], gl[line, column] = split(block)
            if index not in (0, 2):
                block = block.T
                gm[column, line] = block
                gh[column, line], gl[column, line] = split(block)

    for part in range(2):
        for k, offset in enumerate(OFFSETS):
            source = gf.at[c, piece(part, plane(((4 - offset[0]) % 4, (4 - offset[1]) % 4)))]
            wait_recv(source, sem_f.at[part, k])
            send_b_now(source, source, sem_s.at[part], sibling)
        place(c, part)
    for part in range(2):
        start, size = PARTS[part]
        wait_recv(gf.at[1 - c, start : start + size], sem_s.at[part])
        place(1 - c, part)

    diag = lax.broadcasted_iota(jnp.int32, (128, 128), 0) == lax.broadcasted_iota(jnp.int32, (128, 128), 1)
    both = (gf[0, 0:128, :] + gf[0, 256:384, :]) + (gf[1, 0:128, :] + gf[1, 256:384, :])
    trace = jnp.sum(jnp.where(diag, both, 0.0), keepdims=True)
    inverse = 1.0 / (jnp.sqrt(trace) + epsilon)
    inverse2 = inverse * inverse

    for chunk in range(R // CHUNK):
        at = slice(chunk * CHUNK, (chunk + 1) * CHUNK)
        squared = dot(gh[at, :], gh[...]) + (dot(gh[at, :], gl[...]) + dot(gl[at, :], gh[...]))
        line = lax.broadcasted_iota(jnp.int32, (CHUNK, R), 0) + chunk * CHUNK
        column = lax.broadcasted_iota(jnp.int32, (CHUNK, R), 1)
        polynomial = jnp.where(line == column, linear_coef, 0.0).astype(F32) + (
            square_coef * gm[at, :] + (quint_coef * squared) * inverse2
        ) * inverse2
        ph[at, :], plo[at, :] = split(polynomial)

    def apply(high, low, vector):
        vh, vl = split(vector)
        wide = dot(high[...], jnp.concatenate([vh, vl], axis=1))
        return wide[:, :COLS] + (wide[:, COLS:] + dot(low[...], vh))

    def apply_second(vector):
        vector = apply(ph, plo, vector)
        vector = apply(gh, gl, vector) * inverse2
        return apply(ph, plo, vector)

    iterate = apply(ph, plo, nest[...] * (inverse * math.sqrt(C)))
    once = apply_second(iterate)
    twice = apply_second(once)
    upd_out[...] = linear_coef * iterate + (square_coef * once + quint_coef * twice)

    momentum_done.wait()
    for copy in sends:
        copy.wait_send()


def finish(mom_ref, upd_ref, mom_out, upd_out, sems):
    stores = [
        pltpu.make_async_copy(mom_ref, mom_out, sems.at[0]),
        pltpu.make_async_copy(upd_ref, upd_out, sems.at[1]),
    ]
    for store in stores:
        store.start()
    for store in stores:
        store.wait()


def local(latents, targets, kv_weight, momentum):
    previous = momentum.reshape(R, COLS)
    dma = pltpu.SemaphoreType.DMA
    any_space = pl.BlockSpec(memory_space=pl.ANY)
    vmem = pl.BlockSpec(memory_space=pltpu.VMEM)
    matrix = jax.ShapeDtypeStruct((R, COLS), F32)
    momentum_new, update = pl.pallas_call(
        kernel,
        out_shape=(matrix, matrix),
        in_specs=[any_space] * 4,
        out_specs=(any_space, vmem),
        scratch_shapes=[
            pltpu.VMEM((CHIPS, 2, QUARTER, R), BF16),
            pltpu.VMEM((CHIPS, 2 * HALF, COLS), BF16),
            pltpu.VMEM((2, CHIPS, HALF, COLS), BF16),
            pltpu.VMEM((2, R, COLS), BF16),
            pltpu.VMEM((2, R, COLS), F32),
            pltpu.VMEM((2, R, COLS), F32),
            pltpu.VMEM((2, R, COLS), F32),
            pltpu.VMEM((2, R, 2 * COLS), BF16),
            pltpu.VMEM((R, COLS), F32),
            pltpu.VMEM((5 * 128, 128), F32),
            *[pltpu.VMEM((CHIPS - 1, size // CHIPS, 128), F32) for _, size in PARTS],
            *[pltpu.VMEM((size // CHIPS, 128), F32) for _, size in PARTS],
            *[pltpu.VMEM((NZ - 1, size // CHIPS, 128), F32) for _, size in PARTS],
            pltpu.VMEM((2, 5 * 128, 128), F32),
            pltpu.VMEM((R, R), F32),
            pltpu.VMEM((R, R), BF16),
            pltpu.VMEM((R, R), BF16),
            pltpu.VMEM((R, R), BF16),
            pltpu.VMEM((R, R), BF16),
            dma((72,)),
            dma((112,)),
            dma((4,)),
            dma((CHIPS,)),
            dma((NX,)),
            dma((NX,)),
            dma,
            dma,
            dma((2, 2)),
            dma((2,)),
            dma((2,)),
            dma((2, CHIPS - 1)),
            dma((2,)),
            dma,
            pltpu.SemaphoreType.REGULAR,
            pltpu.SemaphoreType.REGULAR((3, 2)),
        ],
        compiler_params=pltpu.CompilerParams(
            collective_id=0, has_side_effects=True, vmem_limit_bytes=32 << 20
        ),
        name="muon_step",
    )(*[pltpu.with_memory_space_constraint(v, pltpu.HBM) for v in (latents, targets, kv_weight, previous)])
    momentum_new, update = pl.pallas_call(
        finish,
        out_shape=(matrix, matrix),
        in_specs=[vmem] * 2,
        out_specs=(any_space, any_space),
        scratch_shapes=[dma((2,))],
        compiler_params=pltpu.CompilerParams(vmem_limit_bytes=4 << 20),
        name="finish",
    )(momentum_new, update)
    return momentum_new.reshape(R, 1, COLS), update.reshape(R, 1, COLS)


def solution(mesh):
    return jax.shard_map(
        local,
        mesh=mesh,
        in_specs=(P("dp", None), P("dp", "head"), P(None, "head"), P(None, "head", "dp")),
        out_specs=(P(None, "head", "dp"), P(None, "head", "dp")),
        check_vma=False,
    )
```

```python
import math

import jax
import jax.numpy as jnp
from jax import lax
from jax.experimental import pallas as pl
from jax.experimental.pallas import tpu as pltpu
from jax.sharding import PartitionSpec as P

MESH = pl.DeviceIdType.MESH
F32, BF16 = jnp.float32, jnp.bfloat16

R = 512
C = 32768
TOKENS = 2048
NX = 4
NZ = 8
COLS = 128
HALF = 64
QUARTER = 32
CHIPS = NX * NX
PARTS = ((0, 3 * 128), (3 * 128, 2 * 128))
CHUNK = 256

decay_rate = 0.95
linear_coef = 3.4445
square_coef = -4.775
quint_coef = 2.0315
epsilon = 1e-07

OFFSETS = [(0, 1), (0, 3), (1, 0), (3, 0), (1, 1), (1, 3), (3, 1), (3, 3), (0, 2), (2, 0), (1, 2), (3, 2), (2, 1), (2, 3), (2, 2)]
FAR_FIRST = list(reversed(list(enumerate(OFFSETS))))
DIRECT = ((0, 2), (2, 0), (0, 1), (0, 3), (1, 0), (3, 0))
RING = (1, 3, 2)
ZRING = (4, 3, 5, 2, 6, 1, 7)
BLOCKS = (((0, 0), (256, 256)), ((0, 128), (256, 256)), ((128, 128), (256, 256)), ((0, 256), (128, 0)), ((0, 384), (128, 0)))


def split(value):
    high = value.astype(BF16)
    return high, (value - high.astype(F32)).astype(BF16)


def dot(a, b):
    return jnp.dot(a, b, preferred_element_type=F32)


def dot_nt(a, b):
    return lax.dot_general(a, b, (((1,), (1,)), ((), ())), preferred_element_type=F32)


def dot_tn(a, b):
    return lax.dot_general(a, b, (((0,), (0,)), ((), ())), preferred_element_type=F32)


def kernel(
    lat, tgt, wgt, mom, mom_out, upd_out,
    lbuf, tstage, tbuf, wbuf, mbuf, gown, gsib, xbuf, nest, gs, rbuf0, rbuf1, pz0, pz1, zbuf0, zbuf1, gf, gm, gh, gl, ph, plo,
    send_a, send_b, local_sem, sem_l, sem_lz, sem_t, sem_w, sem_m, sem_g, sem_r, sem_z, sem_f, sem_s, out_sem, ready, word,
):
    chip = lax.axis_index("dp")
    head = lax.axis_index("head")
    x, y = lax.div(chip, NX), lax.rem(chip, NX)
    z, c = lax.div(head, 2), lax.rem(head, 2)
    sibling = (chip, z * 2 + (1 - c))

    def step(p, by):
        return lax.rem(p + by, NX)

    def along_z(by):
        return (chip, lax.rem(z + by, NZ) * 2 + c)

    def plane(offset):
        return step(x, offset[0]) * NX + step(y, offset[1])

    def turned(offset):
        a = jnp.where(c == 0, offset[0], offset[1])
        b = jnp.where(c == 0, offset[1], offset[0])
        return plane((a, b))

    def remote(src, dst, ssem, rsem, device):
        return pltpu.make_async_remote_copy(
            src_ref=src, dst_ref=dst, send_sem=ssem, recv_sem=rsem, device_id=device, device_id_type=MESH
        )

    def wait_recv(ref, sem):
        remote(ref, ref, send_a.at[0], sem, sibling).wait_recv()

    barrier = pltpu.get_barrier_semaphore()
    partners = 1
    for _, offset in FAR_FIRST:
        pl.semaphore_signal(barrier, inc=1, device_id=(plane(offset), head), device_id_type=MESH)
        partners += 1
    for by in (1, NZ - 1):
        pl.semaphore_signal(barrier, inc=1, device_id=along_z(by), device_id_type=MESH)
        partners += 1
    pl.semaphore_signal(barrier, inc=1, device_id=sibling, device_id_type=MESH)

    zp = lax.rem(z, 2)
    block_cols = pl.ds(pl.multiple_of(chip * COLS, COLS), COLS)

    def quarter(of):
        return lat.at[pl.ds(pl.multiple_of(c * HALF + of * QUARTER, QUARTER), QUARTER)]

    own_quarter = pltpu.make_async_copy(quarter(zp), lbuf.at[chip, zp], local_sem.at[2])
    own_quarter.start()
    for to in range(CHIPS):
        pltpu.make_async_copy(tgt.at[:, to * COLS : (to + 1) * COLS], tstage.at[to], local_sem.at[0]).start()
    own_weight = pltpu.make_async_copy(wgt.at[:, block_cols], wbuf.at[0], local_sem.at[1])
    own_weight.start()
    pltpu.make_async_copy(quarter(1 - zp), lbuf.at[chip, 1 - zp], sem_lz.at[x]).start()
    own_momentum = pltpu.make_async_copy(mom, mbuf.at[0], local_sem.at[3])
    own_momentum.start()
    pl.semaphore_wait(barrier, partners)
    pl.semaphore_signal(ready, inc=1, device_id=sibling, device_id_type=MESH)

    def tell_z(turn):
        pl.semaphore_signal(word.at[turn, 0], inc=1, device_id=along_z(1), device_id_type=MESH)
        pl.semaphore_signal(word.at[turn, 1], inc=1, device_id=along_z(NZ - 1), device_id_type=MESH)

    def hear_z(turn):
        pl.semaphore_wait(word.at[turn, 0], 1)
        pl.semaphore_wait(word.at[turn, 1], 1)

    sends = []
    count_a = [0]

    def drain():
        while sends:
            sends.pop(0).wait_send()

    def send_now(src, dst, rsem, device):
        copy = remote(src, dst, send_a.at[count_a[0]], rsem, device)
        count_a[0] += 1
        copy.start()
        sends.append(copy)

    own_quarter.wait()
    for offset in DIRECT:
        send_now(lbuf.at[chip, zp], lbuf.at[chip, zp], sem_l.at[chip], (turned(offset), head))

    pltpu.make_async_copy(tstage, tstage, local_sem.at[0]).wait()
    my_rows = pl.ds(pl.multiple_of(c * HALF, HALF), HALF)
    sib_rows = pl.ds(pl.multiple_of((1 - c) * HALF, HALF), HALF)
    own_weight.wait()
    send_now(wbuf.at[0], wbuf.at[1], sem_w, sibling)
    send_now(tstage.at[chip, sib_rows], tbuf.at[1, chip], sem_t.at[x], sibling)
    send_now(mom, mbuf.at[1], sem_m, sibling)
    pltpu.make_async_copy(tstage.at[chip, my_rows], tbuf.at[0, chip], sem_t.at[x]).start()

    flip = [0]

    def swap(slot):
        side = 1 if flip[0] % 2 == 0 else NZ - 1
        flip[0] += 1
        send_now(lbuf.at[slot, zp], lbuf.at[slot, zp], sem_lz.at[lax.div(slot, NX)], along_z(side))

    def arrival(offset, passed_to=()):
        slot = turned(offset)
        wait_recv(lbuf.at[slot, zp], sem_l.at[slot])
        for onward in passed_to:
            send_now(lbuf.at[slot, zp], lbuf.at[slot, zp], sem_l.at[slot], (turned(onward), head))
        swap(slot)

    arrival((0, 1), ((1, 0), (3, 0)))
    arrival((0, 3), ((1, 0), (3, 0)))
    arrival((0, 2), ((2, 0), (1, 0), (3, 0)))
    arrival((2, 0), ((0, 1), (0, 3)))
    arrival((1, 0))
    arrival((3, 0))
    for _, offset in FAR_FIRST:
        to = plane(offset)
        send_now(tstage.at[to, my_rows], tbuf.at[0, chip], sem_t.at[x], (to, head))
    tell_z(0)
    pl.semaphore_wait(ready, 1)
    for _, offset in FAR_FIRST:
        to = plane(offset)
        send_now(tstage.at[to, sib_rows], tbuf.at[1, chip], sem_t.at[x], (to, z * 2 + (1 - c)))
    for offset in OFFSETS[4:8] + OFFSETS[10:]:
        arrival(offset)

    hear_z(0)
    tell_z(1)
    wait_recv(wbuf.at[1], sem_w)
    tokens = NX * HALF

    def group_of(by):
        return pl.ds(step(x, by) * NX, NX)

    def residual_of(by):
        group = group_of(by)
        wait_recv(tbuf.at[:, group], sem_t.at[step(x, by)])
        wait_recv(lbuf.at[group, 1 - zp], sem_lz.at[step(x, by)])
        weight = jnp.concatenate([wbuf[0], wbuf[1]], axis=1)
        target = jnp.concatenate([tbuf[0, group].reshape(tokens, COLS), tbuf[1, group].reshape(tokens, COLS)], axis=1)
        return (dot(lbuf[group].reshape(tokens, R), weight) - target.astype(F32)).astype(BF16)

    def add_gradient(by, residual, first):
        latent = lbuf[group_of(by)].reshape(tokens, R)
        part = dot_tn(latent, residual)
        for r in range(2):
            value = part[:, r * COLS : (r + 1) * COLS]
            if first:
                gown[r] = value
            else:
                gown[r] += value

    add_gradient(0, residual_of(0), True)
    hear_z(1)
    tell_z(2)
    add_gradient(1, residual_of(1), False)
    add_gradient(3, residual_of(3), False)

    residual = residual_of(2)

    def chunk_at(of):
        return pl.ds(pl.multiple_of(of * CHUNK, CHUNK), CHUNK)

    for order, at in enumerate((chunk_at(1 - c), chunk_at(c))):
        part = dot_tn(lbuf[group_of(2), :, :, at].reshape(tokens, CHUNK), residual)
        for r in range(2):
            gown[r, at, :] += part[:, r * COLS : (r + 1) * COLS]
            send_now(gown.at[r, at], gsib.at[1 - r, at], sem_g.at[order, r], sibling)
    wait_recv(mbuf.at[1], sem_m)
    own_momentum.wait()

    def nesterov_of(order, at):
        for r in range(2):
            wait_recv(gsib.at[r, at], sem_g.at[order, 1 - r])
            gradient = (gown[r, at, :] + gsib[r, at, :]) * (1.0 / math.sqrt(TOKENS))
            momentum_new = decay_rate * mbuf[r, at, :] + gradient
            nesterov = gradient + decay_rate * momentum_new
            if r == 0:
                mbuf[0, at, :] = momentum_new
                nest[at, :] = nesterov
            xbuf[0, at, r * COLS : (r + 1) * COLS], xbuf[1, at, r * COLS : (r + 1) * COLS] = split(nesterov)

    def rows(start, size):
        at = pl.ds(pl.multiple_of(start, 128), size)
        return xbuf[0, at, :], xbuf[1, at, :]

    def gram(a, b):
        (ah, al), (bh, bl) = a, b
        return dot_nt(ah, bh) + (dot_nt(ah, bl) + dot_nt(al, bh))

    def piece(part, of):
        size = PARTS[part][1] // CHIPS
        return pl.ds(pl.multiple_of(PARTS[part][0] + of * size, 8), size)

    count_b = [0]

    def send_b_now(src, dst, rsem, device):
        copy = remote(src, dst, send_b.at[count_b[0]], rsem, device)
        count_b[0] += 1
        copy.start()
        sends.append(copy)

    received, summed, over_z = (rbuf0, rbuf1), (pz0, pz1), (zbuf0, zbuf1)

    def scatter(part):
        for k, offset in FAR_FIRST:
            to = plane(offset)
            send_b_now(gs.at[piece(part, to)], received[part].at[k], sem_r.at[part], (to, head))

    hear_z(2)
    nesterov_of(0, chunk_at(c))
    square = rows(c * CHUNK, CHUNK)
    diagonal = gram(square, square)
    gs[0:128, :] = diagonal[:128, :128]
    gs[128:256, :] = diagonal[:128, 128:]
    gs[256:384, :] = diagonal[128:, 128:]
    scatter(0)
    nesterov_of(1, chunk_at(1 - c))
    upper = gram(rows(c * 128, 128), rows(256, 256))
    gs[384:512, :] = upper[:, :128]
    gs[512:640, :] = upper[:, 128:]
    scatter(1)
    momentum_done = pltpu.make_async_copy(mbuf.at[0], mom_out, out_sem)
    momentum_done.start()

    drain()
    for part in range(2):
        wait_recv(received[part], sem_r.at[part])
        total = gs[piece(part, chip), :]
        for k in range(CHIPS - 1):
            total = total + received[part][k]
        summed[part][...] = total
        for by in ZRING:
            send_b_now(summed[part], over_z[part].at[by - 1], sem_z.at[part], along_z(by))
    drain()
    for part in range(2):
        wait_recv(over_z[part], sem_z.at[part])
        total = summed[part][...]
        for k in range(NZ - 1):
            total = total + over_z[part][k]
        mine = gf.at[c, piece(part, chip)]
        gf[c, piece(part, chip), :] = total
        for k, offset in FAR_FIRST:
            send_b_now(mine, mine, sem_f.at[part, k], (plane(offset), head))
        send_b_now(mine, mine, sem_s.at[part], sibling)

    drain()

    def place(half, part):
        for index in ((0, 1, 2), (3, 4))[part]:
            base, more = BLOCKS[index]
            line = pl.ds(pl.multiple_of(base[0] + half * more[0], 128), 128)
            column = pl.ds(pl.multiple_of(base[1] + half * more[1], 128), 128)
            block = gf[half, index * 128 : (index + 1) * 128, :]
            gm[line, column] = block
            gh[line, column], gl[line, column] = split(block)
            if index not in (0, 2):
                block = block.T
                gm[column, line] = block
                gh[column, line], gl[column, line] = split(block)

    for part in range(2):
        for k, offset in enumerate(OFFSETS):
            source = gf.at[c, piece(part, plane(((4 - offset[0]) % 4, (4 - offset[1]) % 4)))]
            wait_recv(source, sem_f.at[part, k])
            send_b_now(source, source, sem_s.at[part], sibling)
        place(c, part)
    drain()
    for part in range(2):
        start, size = PARTS[part]
        wait_recv(gf.at[1 - c, start : start + size], sem_s.at[part])
        place(1 - c, part)

    diag = lax.broadcasted_iota(jnp.int32, (128, 128), 0) == lax.broadcasted_iota(jnp.int32, (128, 128), 1)
    both = (gf[0, 0:128, :] + gf[0, 256:384, :]) + (gf[1, 0:128, :] + gf[1, 256:384, :])
    trace = jnp.sum(jnp.where(diag, both, 0.0), keepdims=True)
    inverse = 1.0 / (jnp.sqrt(trace) + epsilon)
    inverse2 = inverse * inverse

    for chunk in range(R // CHUNK):
        at = slice(chunk * CHUNK, (chunk + 1) * CHUNK)
        squared = dot(gh[at, :], gh[...]) + (dot(gh[at, :], gl[...]) + dot(gl[at, :], gh[...]))
        line = lax.broadcasted_iota(jnp.int32, (CHUNK, R), 0) + chunk * CHUNK
        column = lax.broadcasted_iota(jnp.int32, (CHUNK, R), 1)
        polynomial = jnp.where(line == column, linear_coef, 0.0).astype(F32) + (
            square_coef * gm[at, :] + (quint_coef * squared) * inverse2
        ) * inverse2
        ph[at, :], plo[at, :] = split(polynomial)

    def apply(high, low, vector):
        vh, vl = split(vector)
        wide = dot(high[...], jnp.concatenate([vh, vl], axis=1))
        return wide[:, :COLS] + (wide[:, COLS:] + dot(low[...], vh))

    def apply_second(vector):
        vector = apply(ph, plo, vector)
        vector = apply(gh, gl, vector) * inverse2
        return apply(ph, plo, vector)

    iterate = apply(ph, plo, nest[...] * (inverse * math.sqrt(C)))
    once = apply_second(iterate)
    twice = apply_second(once)
    upd_out[...] = linear_coef * iterate + (square_coef * once + quint_coef * twice)

    momentum_done.wait()


def finish(mom_ref, upd_ref, mom_out, upd_out, sems):
    stores = [
        pltpu.make_async_copy(mom_ref, mom_out, sems.at[0]),
        pltpu.make_async_copy(upd_ref, upd_out, sems.at[1]),
    ]
    for store in stores:
        store.start()
    for store in stores:
        store.wait()


def local(latents, targets, kv_weight, momentum):
    previous = momentum.reshape(R, COLS)
    dma = pltpu.SemaphoreType.DMA
    any_space = pl.BlockSpec(memory_space=pl.ANY)
    vmem = pl.BlockSpec(memory_space=pltpu.VMEM)
    matrix = jax.ShapeDtypeStruct((R, COLS), F32)
    momentum_new, update = pl.pallas_call(
        kernel,
        out_shape=(matrix, matrix),
        in_specs=[any_space] * 4,
        out_specs=(any_space, vmem),
        scratch_shapes=[
            pltpu.VMEM((CHIPS, 2, QUARTER, R), BF16),
            pltpu.VMEM((CHIPS, 2 * HALF, COLS), BF16),
            pltpu.VMEM((2, CHIPS, HALF, COLS), BF16),
            pltpu.VMEM((2, R, COLS), BF16),
            pltpu.VMEM((2, R, COLS), F32),
            pltpu.VMEM((2, R, COLS), F32),
            pltpu.VMEM((2, R, COLS), F32),
            pltpu.VMEM((2, R, 2 * COLS), BF16),
            pltpu.VMEM((R, COLS), F32),
            pltpu.VMEM((5 * 128, 128), F32),
            *[pltpu.VMEM((CHIPS - 1, size // CHIPS, 128), F32) for _, size in PARTS],
            *[pltpu.VMEM((size // CHIPS, 128), F32) for _, size in PARTS],
            *[pltpu.VMEM((NZ - 1, size // CHIPS, 128), F32) for _, size in PARTS],
            pltpu.VMEM((2, 5 * 128, 128), F32),
            pltpu.VMEM((R, R), F32),
            pltpu.VMEM((R, R), BF16),
            pltpu.VMEM((R, R), BF16),
            pltpu.VMEM((R, R), BF16),
            pltpu.VMEM((R, R), BF16),
            dma((72,)),
            dma((112,)),
            dma((4,)),
            dma((CHIPS,)),
            dma((NX,)),
            dma((NX,)),
            dma,
            dma,
            dma((2, 2)),
            dma((2,)),
            dma((2,)),
            dma((2, CHIPS - 1)),
            dma((2,)),
            dma,
            pltpu.SemaphoreType.REGULAR,
            pltpu.SemaphoreType.REGULAR((3, 2)),
        ],
        compiler_params=pltpu.CompilerParams(
            collective_id=0, has_side_effects=True, vmem_limit_bytes=32 << 20
        ),
        name="muon_step",
    )(*[pltpu.with_memory_space_constraint(v, pltpu.HBM) for v in (latents, targets, kv_weight, previous)])
    momentum_new, update = pl.pallas_call(
        finish,
        out_shape=(matrix, matrix),
        in_specs=[vmem] * 2,
        out_specs=(any_space, any_space),
        scratch_shapes=[dma((2,))],
        compiler_params=pltpu.CompilerParams(vmem_limit_bytes=4 << 20),
        name="finish",
    )(momentum_new, update)
    return momentum_new.reshape(R, 1, COLS), update.reshape(R, 1, COLS)


def solution(mesh):
    return jax.shard_map(
        local,
        mesh=mesh,
        in_specs=(P("dp", None), P("dp", "head"), P(None, "head"), P(None, "head", "dp")),
        out_specs=(P(None, "head", "dp"), P(None, "head", "dp")),
        check_vma=False,
    )
```
